128 devices in a mesh: section: 8 (over z, core), space: 16 (over y, x).
Axes of the slice: x: 4, y: 4, z: 4, core: 2. Of those that a mesh axis runs over, the one named last changes fastest.
Arguments:
- inputs: bfloat16 [4, 64, 16, 2, 128], P(None, None, 'space'), may hold values from -6 to 6
- cotangent: bfloat16 [4, 64, 16, 2, 128], P(None, None, 'space'), may hold values from -6 to 6
- conv_weight: bfloat16 [2, 8, 128, 1728], P(None, 'section'), may hold values from -0.15625 to 0.15625
- mix_weight: bfloat16 [2, 8, 64, 128], P(None, 'section'), may hold values from -0.5 to 0.5
Outputs:
- conv_grad: float32 [2, 8, 128, 1728], P(None, 'section')
- mix_grad: float32 [2, 8, 64, 128], P(None, 'section')
The draws below stay inside these ranges and needn't reach their ends.
All inputs are finite; a program needn't handle non-finite values.
Results may differ from the reference program's by a relative error of at most 0.03.
Values may be sent and summed in bfloat16 or wider, within the bound.
A program may use at most 64 MiB of HBM per device.

```python
import math
import jax
import jax.numpy as jnp
from jax import lax

CH = 64
HID = 128
NZ = 128
NY = 2
MB = 4
V = 2
SECTIONS = 8
NX = 16


def block_levels(rng, extent, cuts, least, high):
    def one(dim, shards_of):
        draws = jax.random.uniform(jax.random.fold_in(jax.random.fold_in(rng, 6), dim), (shards_of,), jnp.float32, least / len(cuts), high / len(cuts))
        return jnp.repeat(jnp.exp(draws), extent[dim] // shards_of).reshape((-1,) + (1,) * (len(extent) - dim - 1))

    factor_of = one(*cuts[0])
    for cut in cuts[1:]:
        factor_of = factor_of * one(*cut)
    return factor_of


def noise(rng, dims, scale, most, split=(), held_as=jnp.bfloat16):
    entries = jax.random.normal(rng, dims, jnp.float32) * scale
    if len(split) > 0:
        entries = block_levels(rng, dims, split, -0.22, 0.18) * entries
    return jnp.clip(entries, min=-most, max=most).astype(held_as)


def setup_inputs(seed: int = 0) -> dict:
    seeds = jax.random.split(jax.random.key(seed), 5)
    return {
        "inputs": noise(seeds[0], (MB, CH, NX, NY, NZ), 1.0, 6.0, ((2, 16),)),
        "cotangent": noise(seeds[1], (MB, CH, NX, NY, NZ), 1.0, 6.0, ((2, 16),)),
        "conv_weight": noise(seeds[2], (V, SECTIONS, HID, 27 * CH), (27 * CH) ** -0.5, 0.15625, ((1, 8),)),
        "mix_weight": noise(seeds[3], (V, SECTIONS, CH, HID), HID ** -0.5, 0.5, ((1, 8),)),
    }


def columns(padded, flip_sign, extent_x, extent_y, extent_z):
    pieces = []
    for step_x in (-1, 0, 1):
        for step_y in (-1, 0, 1):
            for step_z in (-1, 0, 1):
                start_x = 1 + flip_sign * step_x
                start_y = 1 + flip_sign * step_y
                start_z = 1 + flip_sign * step_z
                pieces.append(padded[:, start_x:start_x + extent_x, start_y:start_y + extent_y, start_z:start_z + extent_z])
    stacked = jnp.stack(pieces, 0)
    return stacked.reshape(27 * padded.shape[0], extent_x * extent_y * extent_z)

def silu_slope(preact):
    sigmoid_val = jax.nn.sigmoid(preact)
    return sigmoid_val * (1.0 + preact * (1.0 - sigmoid_val))

def transpose_conv(conv_w, channels):
    hidden_count = conv_w.shape[0]
    return conv_w.reshape(hidden_count, 27, channels).transpose(2, 1, 0).reshape(channels, 27 * hidden_count)

def padded_of(field):
    return jnp.pad(field, ((0, 0), (1, 1), (1, 1), (1, 1)))

def reference(inputs, cotangent, conv_weight, mix_weight):
    layer_groups = conv_weight.shape[0]
    section_count = conv_weight.shape[1]
    layer_count = layer_groups * section_count
    conv_all = conv_weight.reshape(layer_count, HID, 27 * CH)
    mix_all = mix_weight.reshape(layer_count, CH, HID)
    cell_count = NX * NY * NZ

    def forward_step(activation, weights):
        conv_w, mix_w = weights
        act_low = activation.astype(jnp.bfloat16)
        window = columns(padded_of(act_low), 1, NX, NY, NZ)
        preact = jnp.dot(conv_w, window, preferred_element_type=jnp.float32)
        hidden = jax.nn.silu(preact).astype(jnp.bfloat16)
        mixed_term = jnp.dot(mix_w, hidden, preferred_element_type=jnp.float32)
        result = activation.reshape(CH, cell_count) + mixed_term
        return (result.reshape(CH, NX, NY, NZ), act_low)

    def backward_step(upstream, layer_pack):
        conv_w, mix_w, act_low = layer_pack
        window = columns(padded_of(act_low), 1, NX, NY, NZ)
        preact = jnp.dot(conv_w, window, preferred_element_type=jnp.float32)
        hidden = jax.nn.silu(preact).astype(jnp.bfloat16)
        flat_up = upstream.reshape(CH, cell_count)
        up_low = flat_up.astype(jnp.bfloat16)
        mix_term = jnp.dot(up_low, hidden.T, preferred_element_type=jnp.float32)
        hid_grad = jnp.dot(mix_w.T, up_low, preferred_element_type=jnp.float32)
        pre_grad = (hid_grad * silu_slope(preact)).astype(jnp.bfloat16)
        conv_term = jnp.dot(pre_grad, window.T, preferred_element_type=jnp.float32)
        back_window = columns(padded_of(pre_grad.reshape(HID, NX, NY, NZ)), -1, NX, NY, NZ)
        spread = jnp.dot(transpose_conv(conv_w, CH), back_window, preferred_element_type=jnp.float32)
        downstream = flat_up + spread
        return (downstream.reshape(CH, NX, NY, NZ), (conv_term, mix_term))

    def one_micro(totals, micro_pair):
        source, seed_grad = micro_pair
        final_act, saved = lax.scan(forward_step, source.astype(jnp.float32), (conv_all, mix_all))
        first_up, layer_terms = lax.scan(backward_step, seed_grad.astype(jnp.float32), (conv_all, mix_all, saved), reverse=True)
        return ((totals[0] + layer_terms[0], totals[1] + layer_terms[1]), None)
    start_totals = (jnp.zeros((layer_count, HID, 27 * CH), jnp.float32), jnp.zeros((layer_count, CH, HID), jnp.float32))
    totals, unused = lax.scan(one_micro, start_totals, (inputs, cotangent))
    factor = 1.0 / math.sqrt(MB * NX * NY * NZ)
    conv_grad = (totals[0] * factor).reshape(layer_groups, section_count, HID, 27 * CH)
    mix_grad = (totals[1] * factor).reshape(layer_groups, section_count, CH, HID)
    return (conv_grad, mix_grad)
```

```python
import functools
import math

import jax
import jax.numpy as jnp
from jax import lax
from jax.experimental import pallas as pl
from jax.experimental.pallas import tpu as pltpu
from jax.sharding import PartitionSpec as P

NZ = 128
PLANES = 8
BLOCKS = 16
KC = 128
HC = 256
F32 = jnp.float32
BF16 = jnp.bfloat16
MESH = pl.DeviceIdType.MESH
NT = (((1,), (1,)), ((), ()))
TN = (((0,), (0,)), ((), ()))
FWD_CHUNKS = ((1, 2), (3, 2), (5, 3))
BWD_CHUNKS = ((1, 2), (3, 2), (5, 3))


def rows_of(start, count):
    return pl.ds(pl.multiple_of(start * NZ, NZ), count * NZ)


def shifted(value, step):
    planes = value.shape[0] // NZ
    rolled = pltpu.roll(value, (-step) % value.shape[0], 0)
    row = lax.broadcasted_iota(jnp.int32, value.shape, 0) % NZ
    edge = NZ - 1 if step == 1 else 0
    return jnp.where(row == edge, 0.0, rolled)


def widen(value):
    return jnp.concatenate(
        [shifted(value, -1).astype(BF16), value.astype(BF16), shifted(value, 1).astype(BF16)], axis=1
    )


def chain_kernel(
    block_shift,
    x_ref, cot_ref, w_ref, mf_ref, mb_ref,
    g_ref, gm_ref,
    a3a, a3b, act, slope, sa3, shid, pga, pgb,
    fsend, frecv, bsend, brecv,
):
    section = lax.axis_index("section")
    core = lax.rem(section, 2)
    partner = section + 1 - 2 * core
    mine = lax.axis_index("space") + block_shift
    sign = 2 * core - 1

    def globally(local):
        return 7 + core + sign * local

    zeros3 = jnp.zeros((NZ, 3 * KC), BF16)
    for a3 in (a3a, a3b):
        a3[9 * NZ : 10 * NZ, :] = zeros3
    for pg in (pga, pgb):
        pg[9 * NZ : 10 * NZ, :] = jnp.zeros((NZ, HC), BF16)
    for local in range(-1, PLANES):
        tile = x_ref[globally(local)].astype(F32)
        if local >= 0:
            act[local * NZ : (local + 1) * NZ, :] = tile
        a3a[(local + 1) * NZ : (local + 2) * NZ, :] = widen(tile)

    def forward_planes(cur, nxt, block, first, count):
        rows = slice(first * NZ, (first + count) * NZ)
        window = jnp.concatenate(
            [
                cur[rows_of(first + 1 - sign, count), :],
                cur[(first + 1) * NZ : (first + 1 + count) * NZ, :],
                cur[rows_of(first + 1 + sign, count), :],
            ],
            axis=1,
        )
        pre = jnp.dot(window, w_ref[block], preferred_element_type=F32)
        sg = 0.5 + 0.5 * jnp.tanh(0.5 * pre)
        hid = pre * sg
        slope[block, rows, :] = (sg + hid * (1.0 - sg)).astype(BF16)
        hid = hid.astype(BF16)

        @pl.when(block == mine)
        def _():
            shid[rows, :] = hid

        new = act[rows, :] + jnp.dot(hid, mf_ref[block], preferred_element_type=F32)
        act[rows, :] = new
        nxt[(first + 1) * NZ : (first + 1 + count) * NZ, :] = widen(new)

    def act_copy(buf, par):
        return pltpu.make_async_remote_copy(
            src_ref=buf.at[pl.ds(NZ, NZ)],
            dst_ref=buf.at[pl.ds(0, NZ)],
            send_sem=fsend.at[par],
            recv_sem=frecv.at[par],
            device_id={"section": partner},
            device_id_type=MESH,
        )

    def forward_block(block, cur, nxt, par, wait, send):
        for first, count in FWD_CHUNKS:
            forward_planes(cur, nxt, block, first, count)
        wait(lambda: act_copy(cur, par).wait())

        @pl.when(block == mine)
        def _():
            sa3[...] = cur[...]

        forward_planes(cur, nxt, block, 0, 1)
        send(lambda: act_copy(nxt, 1 - par).start())

    def always(go):
        go()

    def forward_pair(step, carry):
        forward_block(2 * step, a3a, a3b, 0, lambda go: pl.when(step > 0)(go), always)
        forward_block(2 * step + 1, a3b, a3a, 1, always, lambda go: pl.when(step < 7)(go))
        return carry

    lax.fori_loop(0, BLOCKS // 2, forward_pair, 0)

    for local in range(PLANES):
        act[local * NZ : (local + 1) * NZ, :] = cot_ref[globally(local)].astype(F32)

    def backward_prep(pg, block, first, count):
        rows = slice(first * NZ, (first + count) * NZ)
        grad = jnp.dot(act[rows, :].astype(BF16), mb_ref[block], preferred_element_type=F32)
        pg[(first + 1) * NZ : (first + 1 + count) * NZ, :] = (
            grad * slope[block, rows, :].astype(F32)
        ).astype(BF16)

    def backward_planes(pg, block, first, count):
        rows = slice(first * NZ, (first + count) * NZ)
        spread = (
            lax.dot_general(
                pg[rows_of(first + 1 + sign, count), :], w_ref[block, 0:384], NT,
                preferred_element_type=F32,
            )
            + lax.dot_general(
                pg[(first + 1) * NZ : (first + 1 + count) * NZ, :], w_ref[block, 384:768], NT,
                preferred_element_type=F32,
            )
            + lax.dot_general(
                pg[rows_of(first + 1 - sign, count), :], w_ref[block, 768:1152], NT,
                preferred_element_type=F32,
            )
        )
        act[rows, :] = act[rows, :] + (
            shifted(spread[:, 0:128], 1) + spread[:, 128:256] + shifted(spread[:, 256:384], -1)
        )

    def grad_copy(buf, par):
        return pltpu.make_async_remote_copy(
            src_ref=buf.at[pl.ds(NZ, NZ)],
            dst_ref=buf.at[pl.ds(0, NZ)],
            send_sem=bsend.at[par],
            recv_sem=brecv.at[par],
            device_id={"section": partner},
            device_id_type=MESH,
        )

    def backward_block(block, pg, par, last):
        backward_prep(pg, block, 0, 1)
        last(lambda: grad_copy(pg, par).start())
        for first, count in BWD_CHUNKS:
            backward_prep(pg, block, first, count)

        @pl.when(block == mine)
        def _():
            own = pg[NZ : 9 * NZ, :]
            for dx in range(3):
                g_ref[:, dx * 384 : (dx + 1) * 384] = lax.dot_general(
                    own, sa3[rows_of(1 + (dx - 1) * sign, PLANES), :], TN,
                    preferred_element_type=F32,
                )
            gm_ref[...] = lax.dot_general(
                act[...].astype(BF16), shid[...], TN, preferred_element_type=F32
            )

        def rest():
            for first, count in BWD_CHUNKS:
                backward_planes(pg, block, first, count)
            grad_copy(pg, par).wait()
            backward_planes(pg, block, 0, 1)

        last(rest)

    def backward_pair(step, carry):
        backward_block(15 - 2 * step, pga, 0, always)
        backward_block(14 - 2 * step, pgb, 1, lambda go: pl.when(step < 7)(go))
        return carry

    lax.fori_loop(0, BLOCKS // 2, backward_pair, 0)


def run_chain(x, cot, w, mf, mb, block_shift=0):
    vmem = pl.BlockSpec(memory_space=pltpu.VMEM)
    return pl.pallas_call(
        functools.partial(chain_kernel, block_shift),
        out_shape=(
            jax.ShapeDtypeStruct((HC, 9 * KC), F32),
            jax.ShapeDtypeStruct((KC, HC), F32),
        ),
        in_specs=[vmem] * 5,
        out_specs=(vmem, vmem),
        scratch_shapes=[
            pltpu.VMEM((10 * NZ, 3 * KC), BF16),
            pltpu.VMEM((10 * NZ, 3 * KC), BF16),
            pltpu.VMEM((PLANES * NZ, KC), F32),
            pltpu.VMEM((BLOCKS, PLANES * NZ, HC), BF16),
            pltpu.VMEM((10 * NZ, 3 * KC), BF16),
            pltpu.VMEM((PLANES * NZ, HC), BF16),
            pltpu.VMEM((10 * NZ, HC), BF16),
            pltpu.VMEM((10 * NZ, HC), BF16),
            pltpu.SemaphoreType.DMA((2,)),
            pltpu.SemaphoreType.DMA((2,)),
            pltpu.SemaphoreType.DMA((2,)),
            pltpu.SemaphoreType.DMA((2,)),
        ],
        compiler_params=pltpu.CompilerParams(
            has_side_effects=True, vmem_limit_bytes=60 * 1024 * 1024
        ),
        name="chain",
    )(x, cot, w, mf, mb)


def conv_matrix(conv_w):
    taps = conv_w.reshape(-1, 128, 3, 3, 3, 64).transpose(0, 2, 3, 4, 5, 1)
    low, mid, high = taps[:, :, 0], taps[:, :, 1], taps[:, :, 2]
    top = jnp.concatenate([mid, low], axis=-1)
    bottom = jnp.concatenate([high, mid], axis=-1)
    return jnp.stack([top, bottom], axis=3).reshape(-1, 9 * KC, HC)


def mix_matrix(mix_w):
    empty = jnp.zeros_like(mix_w)
    return jnp.concatenate(
        [jnp.concatenate([mix_w, empty], 2), jnp.concatenate([empty, mix_w], 2)], 1
    )


def fold_conv(grad):
    parts = grad.reshape(2, 128, 3, 3, 2, 64)
    mid = parts[0, :, :, :, 0] + parts[1, :, :, :, 1]
    low = parts[1, :, :, :, 0]
    high = parts[0, :, :, :, 1]
    return jnp.stack([low, mid, high], axis=2).reshape(128, 1728)


def fold_mix(grad):
    return grad[0:64, 0:128] + grad[64:128, 128:256]


def plane_rows(tile):
    return tile[:, 0].transpose(2, 1, 0).reshape(NZ, KC)


def per_device(inputs, cotangent, conv_weight, mix_weight):
    section = lax.axis_index("section")
    space = lax.axis_index("space")
    micro = section // 2
    x = plane_rows(lax.dynamic_index_in_dim(inputs, micro, 0, keepdims=False))
    cot = plane_rows(lax.dynamic_index_in_dim(cotangent, micro, 0, keepdims=False))
    both = lax.all_gather(jnp.stack([x, cot], 0), "space")
    w = lax.all_gather(conv_matrix(conv_weight[:, 0]), "section")
    w = w.transpose(1, 0, 2, 3).reshape(BLOCKS, 9 * KC, HC)
    mix = lax.all_gather(mix_weight[:, 0], "section").transpose(1, 0, 2, 3).reshape(BLOCKS, 64, 128)
    mb = mix_matrix(mix)
    mf = mb.transpose(0, 2, 1)
    grad, grad_mix = run_chain(both[:, 0], both[:, 1], w, mf, mb)
    factor = 1.0 / math.sqrt(16384.0)
    part = jnp.concatenate([fold_conv(grad).reshape(-1, 128), fold_mix(grad_mix)], 0) * factor
    part = lax.psum(part, "section")
    slot = jnp.stack(
        [jnp.where(space == section, part, 0.0), jnp.where(space == section + 8, part, 0.0)], 0
    )
    total = lax.psum(slot, "space")
    return (
        total[:, :1728].reshape(2, 1, 128, 1728),
        total[:, 1728:].reshape(2, 1, 64, 128),
    )


def solution(mesh):
    placed = (
        P(None, None, "space", None, None),
        P(None, None, "space", None, None),
        P(None, "section", None, None),
        P(None, "section", None, None),
    )
    return jax.shard_map(
        per_device,
        mesh=mesh,
        in_specs=placed,
        out_specs=(P(None, "section", None, None), P(None, "section", None, None)),
        check_vma=False,
    )
```

```python
import math

import jax
import jax.numpy as jnp
from jax import lax
from jax.experimental import pallas as pl
from jax.experimental.pallas import tpu as pltpu
from jax.sharding import PartitionSpec as P

NZ = 128
PLANES = 8
BLOCKS = 16
KC = 128
HC = 256
F32 = jnp.float32
BF16 = jnp.bfloat16
MESH = pl.DeviceIdType.MESH
NT = (((1,), (1,)), ((), ()))
TN = (((0,), (0,)), ((), ()))
FWD_CHUNKS = ((1, 2), (3, 2), (5, 3))
BWD_CHUNKS = ((1, 2), (3, 2), (5, 3))
SECTIONS = 8
SPACES = 16
TAPS_ROWS = 1728
GRAD_ROWS = 1792
PART = GRAD_ROWS // SECTIONS
FACTOR = 1.0 / math.sqrt(16384.0)


def rows_of(start, count):
    return pl.ds(pl.multiple_of(start * NZ, NZ), count * NZ)


def shifted(value, step):
    planes = value.shape[0] // NZ
    rolled = pltpu.roll(value, (-step) % value.shape[0], 0)
    row = lax.broadcasted_iota(jnp.int32, value.shape, 0) % NZ
    edge = NZ - 1 if step == 1 else 0
    return jnp.where(row == edge, 0.0, rolled)


def widen(value):
    return jnp.concatenate(
        [shifted(value, -1).astype(BF16), value.astype(BF16), shifted(value, 1).astype(BF16)], axis=1
    )


def chain_kernel(
    tile_ref, w_ref, mf_ref, mb_ref,
    conv_ref, mix_ref,
    a3a, a3b, act, slope, sa3, shid, pga, pgb,
    tiles, grad, gsend, gparts, chunk, home,
    fsend, frecv, bsend, brecv,
    tsend, trecv, psend, precv, hsend, hrecv,
):
    section = lax.axis_index("section")
    core = lax.rem(section, 2)
    partner = section + 1 - 2 * core
    mine = lax.axis_index("space")
    sign = 2 * core - 1

    def globally(local):
        return 7 + core + sign * local

    def tile_copy(step, slot):
        return pltpu.make_async_remote_copy(
            src_ref=tile_ref,
            dst_ref=tiles.at[slot],
            send_sem=tsend.at[step],
            recv_sem=trecv.at[slot],
            device_id={"space": lax.rem(mine + step, SPACES)},
            device_id_type=MESH,
        )

    needed = jnp.where(core == 0, mine <= 8, mine >= 7)

    @pl.when(needed)
    def _():
        for step in range(1, SPACES):
            tile_copy(step, mine).start()

    tiles[mine] = tile_ref[...]

    zeros3 = jnp.zeros((NZ, 3 * KC), BF16)
    for a3 in (a3a, a3b):
        a3[9 * NZ : 10 * NZ, :] = zeros3
    for pg in (pga, pgb):
        pg[9 * NZ : 10 * NZ, :] = jnp.zeros((NZ, HC), BF16)
    for local in range(-1, PLANES):
        plane = globally(local)
        pl.when(plane != mine)(lambda plane=plane: tile_copy(1, plane).wait_recv())
        tile = tiles[plane, 0].astype(F32)
        if local >= 0:
            act[local * NZ : (local + 1) * NZ, :] = tile
        a3a[(local + 1) * NZ : (local + 2) * NZ, :] = widen(tile)

    def forward_planes(cur, nxt, block, first, count):
        rows = slice(first * NZ, (first + count) * NZ)
        window = jnp.concatenate(
            [
                cur[rows_of(first + 1 - sign, count), :],
                cur[(first + 1) * NZ : (first + 1 + count) * NZ, :],
                cur[rows_of(first + 1 + sign, count), :],
            ],
            axis=1,
        )
        pre = jnp.dot(window, w_ref[block], preferred_element_type=F32)
        sg = 0.5 + 0.5 * jnp.tanh(0.5 * pre)
        hid = pre * sg
        slope[block, rows, :] = (sg + hid * (1.0 - sg)).astype(BF16)
        hid = hid.astype(BF16)

        @pl.when(block == mine)
        def _():
            shid[rows, :] = hid

        new = act[rows, :] + jnp.dot(hid, mf_ref[block], preferred_element_type=F32)
        act[rows, :] = new
        nxt[(first + 1) * NZ : (first + 1 + count) * NZ, :] = widen(new)

    def act_copy(buf, par):
        return pltpu.make_async_remote_copy(
            src_ref=buf.at[pl.ds(NZ, NZ)],
            dst_ref=buf.at[pl.ds(0, NZ)],
            send_sem=fsend.at[par],
            recv_sem=frecv.at[par],
            device_id={"section": partner},
            device_id_type=MESH,
        )

    def forward_block(block, cur, nxt, par, wait, send):
        for first, count in FWD_CHUNKS:
            forward_planes(cur, nxt, block, first, count)
        wait(lambda: act_copy(cur, par).wait())

        @pl.when(block == mine)
        def _():
            sa3[...] = cur[...]

        forward_planes(cur, nxt, block, 0, 1)
        send(lambda: act_copy(nxt, 1 - par).start())

    def always(go):
        go()

    def forward_pair(step, carry):
        forward_block(2 * step, a3a, a3b, 0, lambda go: pl.when(step > 0)(go), always)
        forward_block(2 * step + 1, a3b, a3a, 1, always, lambda go: pl.when(step < 7)(go))
        return carry

    lax.fori_loop(0, BLOCKS // 2, forward_pair, 0)

    for local in range(PLANES):
        act[local * NZ : (local + 1) * NZ, :] = tiles[globally(local), 1].astype(F32)

    def backward_prep(pg, block, first, count):
        rows = slice(first * NZ, (first + count) * NZ)
        grad = jnp.dot(act[rows, :].astype(BF16), mb_ref[block], preferred_element_type=F32)
        pg[(first + 1) * NZ : (first + 1 + count) * NZ, :] = (
            grad * slope[block, rows, :].astype(F32)
        ).astype(BF16)

    def backward_planes(pg, block, first, count):
        rows = slice(first * NZ, (first + count) * NZ)
        spread = (
            lax.dot_general(
                pg[rows_of(first + 1 + sign, count), :], w_ref[block, 0:384], NT,
                preferred_element_type=F32,
            )
            + lax.dot_general(
                pg[(first + 1) * NZ : (first + 1 + count) * NZ, :], w_ref[block, 384:768], NT,
                preferred_element_type=F32,
            )
            + lax.dot_general(
                pg[rows_of(first + 1 - sign, count), :], w_ref[block, 768:1152], NT,
                preferred_element_type=F32,
            )
        )
        act[rows, :] = act[rows, :] + (
            shifted(spread[:, 0:128], 1) + spread[:, 128:256] + shifted(spread[:, 256:384], -1)
        )

    def grad_copy(buf, par):
        return pltpu.make_async_remote_copy(
            src_ref=buf.at[pl.ds(NZ, NZ)],
            dst_ref=buf.at[pl.ds(0, NZ)],
            send_sem=bsend.at[par],
            recv_sem=brecv.at[par],
            device_id={"section": partner},
            device_id_type=MESH,
        )

    def backward_block(block, pg, par, last):
        backward_prep(pg, block, 0, 1)
        last(lambda: grad_copy(pg, par).start())
        for first, count in BWD_CHUNKS:
            backward_prep(pg, block, first, count)

        @pl.when(block == mine)
        def _():
            own = pg[NZ : 9 * NZ, :]
            for dx in range(3):
                term = lax.dot_general(
                    sa3[rows_of(1 + (dx - 1) * sign, PLANES), :], own, TN,
                    preferred_element_type=F32,
                )
                for dz in range(3):
                    first = term[dz * KC : dz * KC + 64]
                    second = term[dz * KC + 64 : (dz + 1) * KC]
                    folded = (first[:, KC:], first[:, :KC] + second[:, KC:], second[:, :KC])
                    for dy in range(3):
                        tap = 9 * dx + 3 * dy + dz
                        grad[tap * 64 : (tap + 1) * 64, :] = folded[dy]
            term = lax.dot_general(
                act[...].astype(BF16), shid[...], TN, preferred_element_type=F32
            )
            grad[TAPS_ROWS:GRAD_ROWS, :] = term[0:64, :KC] + term[64:128, KC:]
            gsend[...] = grad[...].astype(BF16)

        def rest():
            for first, count in BWD_CHUNKS:
                backward_planes(pg, block, first, count)
            grad_copy(pg, par).wait()
            backward_planes(pg, block, 0, 1)

        last(rest)

    def backward_pair(step, carry):
        backward_block(15 - 2 * step, pga, 0, always)
        backward_block(14 - 2 * step, pgb, 1, lambda go: pl.when(step < 7)(go))
        return carry

    lax.fori_loop(0, BLOCKS // 2, backward_pair, 0)

    def part_rows(index):
        return pl.ds(pl.multiple_of(index * PART, PART), PART)

    def part_copy(step):
        to = lax.rem(section + step, SECTIONS)
        return pltpu.make_async_remote_copy(
            src_ref=gsend.at[part_rows(to)],
            dst_ref=gparts.at[step],
            send_sem=psend.at[step],
            recv_sem=precv.at[step],
            device_id={"section": to},
            device_id_type=MESH,
        )

    for step in range(1, SECTIONS):
        part_copy(step).start()

    @pl.when(needed)
    def _():
        for step in range(1, SPACES):
            tile_copy(step, mine).wait_send()

    total = grad[part_rows(section), :]
    for step in range(1, SECTIONS):
        part_copy(step).wait_recv()
        total = total + gparts[step].astype(F32)
    chunk[...] = (total * FACTOR).astype(BF16)

    owner = lax.rem(mine, SECTIONS)
    place = (mine - owner) + section

    def home_copy(step, slot):
        return pltpu.make_async_remote_copy(
            src_ref=chunk,
            dst_ref=home.at[slot],
            send_sem=hsend.at[step],
            recv_sem=hrecv.at[slot],
            device_id={"section": owner, "space": lax.rem(mine + step, SPACES)},
            device_id_type=MESH,
        )

    for step in range(1, SPACES):
        home_copy(step, place).start()

    @pl.when(section != owner)
    def _():
        home_copy(0, place).start()

    @pl.when(section == owner)
    def _():
        home[place] = chunk[...]

    for step in range(1, SECTIONS):
        part_copy(step).wait_send()

    for slot in range(2 * SECTIONS):
        group, part = slot // SECTIONS, slot % SECTIONS
        here = jnp.logical_and(section == part, mine == group * SECTIONS + section)
        pl.when(jnp.logical_not(here))(lambda slot=slot: home_copy(1, slot).wait_recv())
        value = home[slot].astype(F32)
        rows = min(TAPS_ROWS - part * PART, PART)
        conv_ref[group, part * PART : part * PART + rows, :] = value[:rows]
        if rows < PART:
            mix_ref[group] = value[rows:]

    for step in range(1, SPACES):
        home_copy(step, place).wait_send()
    pl.when(section != owner)(lambda: home_copy(0, place).wait_send())


def run_chain(tile, w, mf, mb):
    vmem = pl.BlockSpec(memory_space=pltpu.VMEM)
    return pl.pallas_call(
        chain_kernel,
        out_shape=(
            jax.ShapeDtypeStruct((2, TAPS_ROWS, 128), F32),
            jax.ShapeDtypeStruct((2, 64, 128), F32),
        ),
        in_specs=[vmem] * 4,
        out_specs=(vmem, vmem),
        scratch_shapes=[
            pltpu.VMEM((10 * NZ, 3 * KC), BF16),
            pltpu.VMEM((10 * NZ, 3 * KC), BF16),
            pltpu.VMEM((PLANES * NZ, KC), F32),
            pltpu.VMEM((BLOCKS, PLANES * NZ, HC), BF16),
            pltpu.VMEM((10 * NZ, 3 * KC), BF16),
            pltpu.VMEM((PLANES * NZ, HC), BF16),
            pltpu.VMEM((10 * NZ, HC), BF16),
            pltpu.VMEM((10 * NZ, HC), BF16),
            pltpu.VMEM((SPACES, 2, NZ, KC), BF16),
            pltpu.VMEM((GRAD_ROWS, 128), F32),
            pltpu.VMEM((GRAD_ROWS, 128), BF16),
            pltpu.VMEM((SECTIONS, PART, 128), BF16),
            pltpu.VMEM((PART, 128), BF16),
            pltpu.VMEM((2 * SECTIONS, PART, 128), BF16),
            pltpu.SemaphoreType.DMA((2,)),
            pltpu.SemaphoreType.DMA((2,)),
            pltpu.SemaphoreType.DMA((2,)),
            pltpu.SemaphoreType.DMA((2,)),
            pltpu.SemaphoreType.DMA((SPACES,)),
            pltpu.SemaphoreType.DMA((SPACES,)),
            pltpu.SemaphoreType.DMA((SECTIONS,)),
            pltpu.SemaphoreType.DMA((SECTIONS,)),
            pltpu.SemaphoreType.DMA((SPACES,)),
            pltpu.SemaphoreType.DMA((2 * SECTIONS,)),
        ],
        compiler_params=pltpu.CompilerParams(
            has_side_effects=True, vmem_limit_bytes=60 * 1024 * 1024
        ),
        name="chain",
    )(tile, w, mf, mb)


def conv_matrix(conv_w):
    taps = conv_w.reshape(-1, 128, 3, 3, 3, 64).transpose(0, 2, 3, 4, 5, 1)
    low, mid, high = taps[:, :, 0], taps[:, :, 1], taps[:, :, 2]
    top = jnp.concatenate([mid, low], axis=-1)
    bottom = jnp.concatenate([high, mid], axis=-1)
    return jnp.stack([top, bottom], axis=3).reshape(-1, 9 * KC, HC)


def mix_matrix(mix_w):
    empty = jnp.zeros_like(mix_w)
    return jnp.concatenate(
        [jnp.concatenate([mix_w, empty], 2), jnp.concatenate([empty, mix_w], 2)], 1
    )


def plane_rows(tile):
    return tile[:, 0].transpose(2, 1, 0).reshape(NZ, KC)


def per_device(inputs, cotangent, conv_weight, mix_weight):
    micro = lax.axis_index("section") // 2
    x = plane_rows(lax.dynamic_index_in_dim(inputs, micro, 0, keepdims=False))
    cot = plane_rows(lax.dynamic_index_in_dim(cotangent, micro, 0, keepdims=False))
    w = lax.all_gather(conv_matrix(conv_weight[:, 0]), "section")
    w = w.transpose(1, 0, 2, 3).reshape(BLOCKS, 9 * KC, HC)
    mix = lax.all_gather(mix_weight[:, 0], "section").transpose(1, 0, 2, 3).reshape(BLOCKS, 64, 128)
    mb = mix_matrix(mix)
    mf = mb.transpose(0, 2, 1)
    conv_grad, mix_grad = run_chain(jnp.stack([x, cot], 0), w, mf, mb)
    return conv_grad.transpose(0, 2, 1)[:, None], mix_grad[:, None]


def solution(mesh):
    placed = (
        P(None, None, "space", None, None),
        P(None, None, "space", None, None),
        P(None, "section", None, None),
        P(None, "section", None, None),
    )
    return jax.shard_map(
        per_device,
        mesh=mesh,
        in_specs=placed,
        out_specs=(P(None, "section", None, None), P(None, "section", None, None)),
        check_vma=False,
    )
```

```python
import math

import jax
import jax.numpy as jnp
from jax import lax
from jax.experimental import pallas as pl
from jax.experimental.pallas import tpu as pltpu
from jax.sharding import PartitionSpec as P

NZ = 128
PLANES = 8
BLOCKS = 16
KC = 128
HC = 256
F32 = jnp.float32
BF16 = jnp.bfloat16
MESH = pl.DeviceIdType.MESH
NT = (((1,), (1,)), ((), ()))
TN = (((0,), (0,)), ((), ()))
FWD_CHUNKS = ((1, 2), (3, 2), (5, 3))
BWD_CHUNKS = ((1, 2), (3, 2), (5, 3))
SECTIONS = 8
SPACES = 16
TAPS_ROWS = 1728
GRAD_ROWS = 1792
PART = GRAD_ROWS // SECTIONS
FACTOR = 1.0 / math.sqrt(16384.0)


def rows_of(start, count):
    return pl.ds(pl.multiple_of(start * NZ, NZ), count * NZ)


def shifted(value, step):
    planes = value.shape[0] // NZ
    rolled = pltpu.roll(value, (-step) % value.shape[0], 0)
    row = lax.broadcasted_iota(jnp.int32, value.shape, 0) % NZ
    edge = NZ - 1 if step == 1 else 0
    return jnp.where(row == edge, 0.0, rolled)


def widen(value):
    return jnp.concatenate(
        [shifted(value, -1).astype(BF16), value.astype(BF16), shifted(value, 1).astype(BF16)], axis=1
    )


def chain_kernel(
    tile_ref, wt_ref, mt_ref,
    conv_ref, mix_ref,
    a3a, a3b, act, slope, sa3, shid, pga, pgb,
    tiles, grad, gsend, gparts, chunk, home,
    wraw, mraw, w_ref, mb_ref,
    fsend, frecv, bsend, brecv,
    tsend, trecv, psend, precv, hsend, hrecv,
    wsend, msend, wrelay, mrelay, wrecv, mrecv,
):
    section = lax.axis_index("section")
    core = lax.rem(section, 2)
    partner = section + 1 - 2 * core
    mine = lax.axis_index("space")
    sign = 2 * core - 1

    def globally(local):
        return 7 + core + sign * local

    def tile_copy(step, slot):
        return pltpu.make_async_remote_copy(
            src_ref=tile_ref,
            dst_ref=tiles.at[slot],
            send_sem=tsend.at[step],
            recv_sem=trecv.at[slot],
            device_id={"space": lax.rem(mine + step, SPACES)},
            device_id_type=MESH,
        )

    needed = jnp.where(core == 0, mine <= 8, mine >= 7)

    @pl.when(needed)
    def _():
        for step in range(1, SPACES):
            tile_copy(step, mine).start()

    def weight_copies(group, hop):
        to = partner if hop == 0 else lax.rem(section + 2 * hop, SECTIONS)
        block = group * SECTIONS + section
        return [
            pltpu.make_async_remote_copy(
                src_ref=src.at[group],
                dst_ref=dst.at[block],
                send_sem=send.at[group, hop],
                recv_sem=recv.at[block],
                device_id={"section": to},
                device_id_type=MESH,
            )
            for src, dst, send, recv in (
                (wt_ref, wraw, wsend, wrecv), (mt_ref, mraw, msend, mrecv)
            )
        ]

    def relay_copies(block):
        return [
            pltpu.make_async_remote_copy(
                src_ref=buf.at[block],
                dst_ref=buf.at[block],
                send_sem=send.at[block],
                recv_sem=recv.at[block],
                device_id={"section": partner},
                device_id_type=MESH,
            )
            for buf, send, recv in ((wraw, wrelay, wrecv), (mraw, mrelay, mrecv))
        ]

    for group in range(2):
        for hop in (0, 1, 3, 2):
            for copy in weight_copies(group, hop):
                copy.start()
        wraw[group * SECTIONS + section] = wt_ref[group]
        mraw[group * SECTIONS + section] = mt_ref[group]

    def relayed_here(block):
        return jnp.logical_and(lax.rem(block, 2) == core, lax.rem(block, SECTIONS) != section)

    def pass_on(block):
        @pl.when(relayed_here(block))
        def _():
            for copy in relay_copies(block):
                copy.wait_recv()
            for copy in relay_copies(block):
                copy.start()

    def expand(block):
        @pl.when(lax.rem(block, 2) != core)
        def _():
            for copy in relay_copies(block):
                copy.wait_recv()

        for dx in range(3):
            for dz in range(3):
                row = (3 * dx + dz) * KC
                low, mid, high = (
                    wraw[block, (9 * dx + 3 * dy + dz) * 64 : (9 * dx + 3 * dy + dz + 1) * 64, :]
                    for dy in range(3)
                )
                w_ref[block, row : row + 64, 0:128] = mid
                w_ref[block, row : row + 64, 128:256] = low
                w_ref[block, row + 64 : row + 128, 0:128] = high
                w_ref[block, row + 64 : row + 128, 128:256] = mid
        empty = jnp.zeros((64, 128), BF16)
        mb_ref[block, 0:64, 0:128] = mraw[block]
        mb_ref[block, 0:64, 128:256] = empty
        mb_ref[block, 64:128, 0:128] = empty
        mb_ref[block, 64:128, 128:256] = mraw[block]

    tiles[mine] = tile_ref[...]
    pass_on(0)
    pass_on(1)

    zeros3 = jnp.zeros((NZ, 3 * KC), BF16)
    for a3 in (a3a, a3b):
        a3[9 * NZ : 10 * NZ, :] = zeros3
    for pg in (pga, pgb):
        pg[9 * NZ : 10 * NZ, :] = jnp.zeros((NZ, HC), BF16)
    for local in range(-1, PLANES):
        plane = globally(local)
        pl.when(plane != mine)(lambda plane=plane: tile_copy(1, plane).wait_recv())
        tile = tiles[plane, 0].astype(F32)
        if local >= 0:
            act[local * NZ : (local + 1) * NZ, :] = tile
        a3a[(local + 1) * NZ : (local + 2) * NZ, :] = widen(tile)

    def forward_planes(cur, nxt, block, first, count):
        rows = slice(first * NZ, (first + count) * NZ)
        window = jnp.concatenate(
            [
                cur[rows_of(first + 1 - sign, count), :],
                cur[(first + 1) * NZ : (first + 1 + count) * NZ, :],
                cur[rows_of(first + 1 + sign, count), :],
            ],
            axis=1,
        )
        pre = jnp.dot(window, w_ref[block], preferred_element_type=F32)
        sg = 0.5 + 0.5 * jnp.tanh(0.5 * pre)
        hid = pre * sg
        slope[block, rows, :] = (sg + hid * (1.0 - sg)).astype(BF16)
        hid = hid.astype(BF16)

        @pl.when(block == mine)
        def _():
            shid[rows, :] = hid

        new = act[rows, :] + lax.dot_general(
            hid, mb_ref[block], NT, preferred_element_type=F32
        )
        act[rows, :] = new
        nxt[(first + 1) * NZ : (first + 1 + count) * NZ, :] = widen(new)

    def act_copy(buf, par):
        return pltpu.make_async_remote_copy(
            src_ref=buf.at[pl.ds(NZ, NZ)],
            dst_ref=buf.at[pl.ds(0, NZ)],
            send_sem=fsend.at[par],
            recv_sem=frecv.at[par],
            device_id={"section": partner},
            device_id_type=MESH,
        )

    def forward_block(block, cur, nxt, par, wait, send):
        expand(block)
        for first, count in FWD_CHUNKS:
            forward_planes(cur, nxt, block, first, count)
        wait(lambda: act_copy(cur, par).wait())

        @pl.when(block == mine)
        def _():
            sa3[...] = cur[...]

        forward_planes(cur, nxt, block, 0, 1)
        send(lambda: act_copy(nxt, 1 - par).start())
        pl.when(block < BLOCKS - 2)(lambda: pass_on(block + 2))

    def always(go):
        go()

    def forward_pair(step, carry):
        forward_block(2 * step, a3a, a3b, 0, lambda go: pl.when(step > 0)(go), always)
        forward_block(2 * step + 1, a3b, a3a, 1, always, lambda go: pl.when(step < 7)(go))
        return carry

    lax.fori_loop(0, BLOCKS // 2, forward_pair, 0)

    for group in range(2):
        for hop in range(4):
            for copy in weight_copies(group, hop):
                copy.wait_send()
    for block in range(BLOCKS):
        @pl.when(relayed_here(block))
        def _(block=block):
            for copy in relay_copies(block):
                copy.wait_send()

    for local in range(PLANES):
        act[local * NZ : (local + 1) * NZ, :] = tiles[globally(local), 1].astype(F32)

    def backward_prep(pg, block, first, count):
        rows = slice(first * NZ, (first + count) * NZ)
        grad = jnp.dot(act[rows, :].astype(BF16), mb_ref[block], preferred_element_type=F32)
        pg[(first + 1) * NZ : (first + 1 + count) * NZ, :] = (
            grad * slope[block, rows, :].astype(F32)
        ).astype(BF16)

    def backward_planes(pg, block, first, count):
        rows = slice(first * NZ, (first + count) * NZ)
        spread = (
            lax.dot_general(
                pg[rows_of(first + 1 + sign, count), :], w_ref[block, 0:384], NT,
                preferred_element_type=F32,
            )
            + lax.dot_general(
                pg[(first + 1) * NZ : (first + 1 + count) * NZ, :], w_ref[block, 384:768], NT,
                preferred_element_type=F32,
            )
            + lax.dot_general(
                pg[rows_of(first + 1 - sign, count), :], w_ref[block, 768:1152], NT,
                preferred_element_type=F32,
            )
        )
        act[rows, :] = act[rows, :] + (
            shifted(spread[:, 0:128], 1) + spread[:, 128:256] + shifted(spread[:, 256:384], -1)
        )

    def grad_copy(buf, par):
        return pltpu.make_async_remote_copy(
            src_ref=buf.at[pl.ds(NZ, NZ)],
            dst_ref=buf.at[pl.ds(0, NZ)],
            send_sem=bsend.at[par],
            recv_sem=brecv.at[par],
            device_id={"section": partner},
            device_id_type=MESH,
        )

    def backward_block(block, pg, par, last):
        backward_prep(pg, block, 0, 1)
        last(lambda: grad_copy(pg, par).start())
        for first, count in BWD_CHUNKS:
            backward_prep(pg, block, first, count)

        @pl.when(block == mine)
        def _():
            own = pg[NZ : 9 * NZ, :]
            for dx in range(3):
                term = lax.dot_general(
                    sa3[rows_of(1 + (dx - 1) * sign, PLANES), :], own, TN,
                    preferred_element_type=F32,
                )
                for dz in range(3):
                    first = term[dz * KC : dz * KC + 64]
                    second = term[dz * KC + 64 : (dz + 1) * KC]
                    folded = (first[:, KC:], first[:, :KC] + second[:, KC:], second[:, :KC])
                    for dy in range(3):
                        tap = 9 * dx + 3 * dy + dz
                        grad[tap * 64 : (tap + 1) * 64, :] = folded[dy]
            term = lax.dot_general(
                act[...].astype(BF16), shid[...], TN, preferred_element_type=F32
            )
            grad[TAPS_ROWS:GRAD_ROWS, :] = term[0:64, :KC] + term[64:128, KC:]
            gsend[...] = grad[...].astype(BF16)

        def rest():
            for first, count in BWD_CHUNKS:
                backward_planes(pg, block, first, count)
            grad_copy(pg, par).wait()
            backward_planes(pg, block, 0, 1)

        last(rest)

    def backward_pair(step, carry):
        backward_block(15 - 2 * step, pga, 0, always)
        backward_block(14 - 2 * step, pgb, 1, lambda go: pl.when(step < 7)(go))
        return carry

    lax.fori_loop(0, BLOCKS // 2, backward_pair, 0)

    def part_rows(index):
        return pl.ds(pl.multiple_of(index * PART, PART), PART)

    def part_copy(step):
        to = lax.rem(section + step, SECTIONS)
        return pltpu.make_async_remote_copy(
            src_ref=gsend.at[part_rows(to)],
            dst_ref=gparts.at[step],
            send_sem=psend.at[step],
            recv_sem=precv.at[step],
            device_id={"section": to},
            device_id_type=MESH,
        )

    for step in range(1, SECTIONS):
        part_copy(step).start()

    @pl.when(needed)
    def _():
        for step in range(1, SPACES):
            tile_copy(step, mine).wait_send()

    total = grad[part_rows(section), :]
    for step in range(1, SECTIONS):
        part_copy(step).wait_recv()
        total = total + gparts[step].astype(F32)
    chunk[...] = (total * FACTOR).astype(BF16)

    owner = lax.rem(mine, SECTIONS)
    place = (mine - owner) + section

    def home_copy(step, slot):
        return pltpu.make_async_remote_copy(
            src_ref=chunk,
            dst_ref=home.at[slot],
            send_sem=hsend.at[step],
            recv_sem=hrecv.at[slot],
            device_id={"section": owner, "space": lax.rem(mine + step, SPACES)},
            device_id_type=MESH,
        )

    for step in range(1, SPACES):
        home_copy(step, place).start()

    @pl.when(section != owner)
    def _():
        home_copy(0, place).start()

    @pl.when(section == owner)
    def _():
        home[place] = chunk[...]

    for step in range(1, SECTIONS):
        part_copy(step).wait_send()

    for slot in range(2 * SECTIONS):
        group, part = slot // SECTIONS, slot % SECTIONS
        here = jnp.logical_and(section == part, mine == group * SECTIONS + section)
        pl.when(jnp.logical_not(here))(lambda slot=slot: home_copy(1, slot).wait_recv())
        value = home[slot].astype(F32)
        rows = min(TAPS_ROWS - part * PART, PART)
        conv_ref[group, part * PART : part * PART + rows, :] = value[:rows]
        if rows < PART:
            mix_ref[group] = value[rows:]

    for step in range(1, SPACES):
        home_copy(step, place).wait_send()
    pl.when(section != owner)(lambda: home_copy(0, place).wait_send())


def run_chain(tile, w, mix):
    vmem = pl.BlockSpec(memory_space=pltpu.VMEM)
    return pl.pallas_call(
        chain_kernel,
        out_shape=(
            jax.ShapeDtypeStruct((2, TAPS_ROWS, 128), F32),
            jax.ShapeDtypeStruct((2, 64, 128), F32),
        ),
        in_specs=[vmem] * 3,
        out_specs=(vmem, vmem),
        scratch_shapes=[
            pltpu.VMEM((10 * NZ, 3 * KC), BF16),
            pltpu.VMEM((10 * NZ, 3 * KC), BF16),
            pltpu.VMEM((PLANES * NZ, KC), F32),
            pltpu.VMEM((BLOCKS, PLANES * NZ, HC), BF16),
            pltpu.VMEM((10 * NZ, 3 * KC), BF16),
            pltpu.VMEM((PLANES * NZ, HC), BF16),
            pltpu.VMEM((10 * NZ, HC), BF16),
            pltpu.VMEM((10 * NZ, HC), BF16),
            pltpu.VMEM((SPACES, 2, NZ, KC), BF16),
            pltpu.VMEM((GRAD_ROWS, 128), F32),
            pltpu.VMEM((GRAD_ROWS, 128), BF16),
            pltpu.VMEM((SECTIONS, PART, 128), BF16),
            pltpu.VMEM((PART, 128), BF16),
            pltpu.VMEM((2 * SECTIONS, PART, 128), BF16),
            pltpu.VMEM((BLOCKS, TAPS_ROWS, 128), BF16),
            pltpu.VMEM((BLOCKS, 64, 128), BF16),
            pltpu.VMEM((BLOCKS, 9 * KC, HC), BF16),
            pltpu.VMEM((BLOCKS, KC, HC), BF16),
            pltpu.SemaphoreType.DMA((2,)),
            pltpu.SemaphoreType.DMA((2,)),
            pltpu.SemaphoreType.DMA((2,)),
            pltpu.SemaphoreType.DMA((2,)),
            pltpu.SemaphoreType.DMA((SPACES,)),
            pltpu.SemaphoreType.DMA((SPACES,)),
            pltpu.SemaphoreType.DMA((SECTIONS,)),
            pltpu.SemaphoreType.DMA((SECTIONS,)),
            pltpu.SemaphoreType.DMA((SPACES,)),
            pltpu.SemaphoreType.DMA((2 * SECTIONS,)),
            pltpu.SemaphoreType.DMA((2, 4)),
            pltpu.SemaphoreType.DMA((2, 4)),
            pltpu.SemaphoreType.DMA((BLOCKS,)),
            pltpu.SemaphoreType.DMA((BLOCKS,)),
            pltpu.SemaphoreType.DMA((BLOCKS,)),
            pltpu.SemaphoreType.DMA((BLOCKS,)),
        ],
        compiler_params=pltpu.CompilerParams(
            has_side_effects=True, vmem_limit_bytes=60 * 1024 * 1024
        ),
        name="chain",
    )(tile, w, mix)


def plane_rows(tile):
    return tile[:, 0].transpose(2, 1, 0).reshape(NZ, KC)


def per_device(inputs, cotangent, conv_weight, mix_weight):
    micro = lax.axis_index("section") // 2
    x = plane_rows(lax.dynamic_index_in_dim(inputs, micro, 0, keepdims=False))
    cot = plane_rows(lax.dynamic_index_in_dim(cotangent, micro, 0, keepdims=False))
    w = conv_weight[:, 0].transpose(0, 2, 1)
    conv_grad, mix_grad = run_chain(jnp.stack([x, cot], 0), w, mix_weight[:, 0])
    return conv_grad.transpose(0, 2, 1)[:, None], mix_grad[:, None]


def solution(mesh):
    placed = (
        P(None, None, "space", None, None),
        P(None, None, "space", None, None),
        P(None, "section", None, None),
        P(None, "section", None, None),
    )
    return jax.shard_map(
        per_device,
        mesh=mesh,
        in_specs=placed,
        out_specs=(P(None, "section", None, None), P(None, "section", None, None)),
        check_vma=False,
    )
```

```python
import math

import jax
import jax.numpy as jnp
from jax import lax
from jax.experimental import pallas as pl
from jax.experimental.pallas import tpu as pltpu
from jax.sharding import PartitionSpec as P

NZ = 128
PLANES = 8
BLOCKS = 16
KC = 128
HC = 256
F32 = jnp.float32
BF16 = jnp.bfloat16
MESH = pl.DeviceIdType.MESH
NT = (((1,), (1,)), ((), ()))
TN = (((0,), (0,)), ((), ()))
FWD_CHUNKS = ((1, 2), (3, 2), (5, 3))
BWD_CHUNKS = ((1, 2), (3, 2), (5, 3))
SECTIONS = 8
SPACES = 16
TAPS_ROWS = 1728
GRAD_ROWS = 1792
PART = GRAD_ROWS // SECTIONS
FACTOR = 1.0 / math.sqrt(16384.0)


def rows_of(start, count):
    return pl.ds(pl.multiple_of(start * NZ, NZ), count * NZ)


def shifted(value, step):
    planes = value.shape[0] // NZ
    rolled = pltpu.roll(value, (-step) % value.shape[0], 0)
    row = lax.broadcasted_iota(jnp.int32, value.shape, 0) % NZ
    edge = NZ - 1 if step == 1 else 0
    return jnp.where(row == edge, 0.0, rolled)


def widen(value):
    return jnp.concatenate(
        [shifted(value, -1).astype(BF16), value.astype(BF16), shifted(value, 1).astype(BF16)], axis=1
    )


def chain_kernel(
    tile_ref, wt_ref, mt_ref,
    conv_ref, mix_ref,
    a3a, a3b, act, slope, sa3, shid, pga, pgb,
    tiles, grad, gsend, gparts, chunk, home,
    wraw, mraw, w_ref, mb_ref,
    fsend, frecv, bsend, brecv,
    tsend, trecv, psend, precv, hsend, hrecv,
    wsend, msend, wrelay, mrelay, wrecv, mrecv,
):
    section = lax.axis_index("section")
    core = lax.rem(section, 2)
    partner = section + 1 - 2 * core
    mine = lax.axis_index("space")
    sign = 2 * core - 1

    def globally(local):
        return 7 + core + sign * local

    def tile_copy(step, slot):
        return pltpu.make_async_remote_copy(
            src_ref=tile_ref,
            dst_ref=tiles.at[slot],
            send_sem=tsend.at[step],
            recv_sem=trecv.at[slot],
            device_id={"space": lax.rem(mine + step, SPACES)},
            device_id_type=MESH,
        )

    needed = jnp.where(core == 0, mine <= 8, mine >= 7)

    @pl.when(needed)
    def _():
        for step in range(1, SPACES):
            tile_copy(step, mine).start()

    def weight_copies(group, hop):
        to = partner if hop == 0 else lax.rem(section + 2 * hop, SECTIONS)
        block = group * SECTIONS + section
        return [
            pltpu.make_async_remote_copy(
                src_ref=src.at[group],
                dst_ref=dst.at[block],
                send_sem=send.at[group, hop],
                recv_sem=recv.at[block],
                device_id={"section": to},
                device_id_type=MESH,
            )
            for src, dst, send, recv in (
                (wt_ref, wraw, wsend, wrecv), (mt_ref, mraw, msend, mrecv)
            )
        ]

    def relay_copies(block):
        return [
            pltpu.make_async_remote_copy(
                src_ref=buf.at[block],
                dst_ref=buf.at[block],
                send_sem=send.at[block],
                recv_sem=recv.at[block],
                device_id={"section": partner},
                device_id_type=MESH,
            )
            for buf, send, recv in ((wraw, wrelay, wrecv), (mraw, mrelay, mrecv))
        ]

    for group in range(2):
        for hop in (0, 1, 3, 2):
            for copy in weight_copies(group, hop):
                copy.start()
        wraw[group * SECTIONS + section] = wt_ref[group]
        mraw[group * SECTIONS + section] = mt_ref[group]

    def relayed_here(block):
        return jnp.logical_and(lax.rem(block, 2) == core, lax.rem(block, SECTIONS) != section)

    def pass_on(block):
        @pl.when(relayed_here(block))
        def _():
            for copy in relay_copies(block):
                copy.wait_recv()
            for copy in relay_copies(block):
                copy.start()

    def expand(block):
        @pl.when(lax.rem(block, 2) != core)
        def _():
            for copy in relay_copies(block):
                copy.wait_recv()

        for dx in range(3):
            for dz in range(3):
                row = (3 * dx + dz) * KC
                low, mid, high = (
                    wraw[block, (9 * dx + 3 * dy + dz) * 64 : (9 * dx + 3 * dy + dz + 1) * 64, :]
                    for dy in range(3)
                )
                w_ref[block, row : row + 64, 0:128] = mid
                w_ref[block, row : row + 64, 128:256] = low
                w_ref[block, row + 64 : row + 128, 0:128] = high
                w_ref[block, row + 64 : row + 128, 128:256] = mid
        empty = jnp.zeros((64, 128), BF16)
        mb_ref[block, 0:64, 0:128] = mraw[block]
        mb_ref[block, 0:64, 128:256] = empty
        mb_ref[block, 64:128, 0:128] = empty
        mb_ref[block, 64:128, 128:256] = mraw[block]

    tiles[mine] = tile_ref[...]
    pass_on(0)
    pass_on(1)

    zeros3 = jnp.zeros((NZ, 3 * KC), BF16)
    for a3 in (a3a, a3b):
        a3[9 * NZ : 10 * NZ, :] = zeros3
    for pg in (pga, pgb):
        pg[9 * NZ : 10 * NZ, :] = jnp.zeros((NZ, HC), BF16)
    for local in range(-1, PLANES):
        plane = globally(local)
        pl.when(plane != mine)(lambda plane=plane: tile_copy(1, plane).wait_recv())
        tile = tiles[plane, 0].astype(F32)
        if local >= 0:
            act[local * NZ : (local + 1) * NZ, :] = tile
        a3a[(local + 1) * NZ : (local + 2) * NZ, :] = widen(tile)

    def forward_planes(cur, nxt, block, first, count):
        rows = slice(first * NZ, (first + count) * NZ)
        window = jnp.concatenate(
            [
                cur[rows_of(first + 1 - sign, count), :],
                cur[(first + 1) * NZ : (first + 1 + count) * NZ, :],
                cur[rows_of(first + 1 + sign, count), :],
            ],
            axis=1,
        )
        pre = jnp.dot(window, w_ref[block], preferred_element_type=F32)
        sg = 0.5 + 0.5 * jnp.tanh(0.5 * pre)
        hid = pre * sg
        slope[block, rows, :] = (sg + hid * (1.0 - sg)).astype(BF16)
        hid = hid.astype(BF16)

        @pl.when(block == mine)
        def _():
            shid[rows, :] = hid

        new = act[rows, :] + lax.dot_general(
            hid, mb_ref[block], NT, preferred_element_type=F32
        )
        act[rows, :] = new
        nxt[(first + 1) * NZ : (first + 1 + count) * NZ, :] = widen(new)

    def act_copy(buf, par):
        return pltpu.make_async_remote_copy(
            src_ref=buf.at[pl.ds(NZ, NZ)],
            dst_ref=buf.at[pl.ds(0, NZ)],
            send_sem=fsend.at[par],
            recv_sem=frecv.at[par],
            device_id={"section": partner},
            device_id_type=MESH,
        )

    def forward_block(block, cur, nxt, par, wait, send):
        expand(block)
        for first, count in FWD_CHUNKS:
            forward_planes(cur, nxt, block, first, count)
        wait(lambda: act_copy(cur, par).wait())

        @pl.when(block == mine)
        def _():
            sa3[...] = cur[...]

        forward_planes(cur, nxt, block, 0, 1)
        send(lambda: act_copy(nxt, 1 - par).start())
        pl.when(block < BLOCKS - 2)(lambda: pass_on(block + 2))

    def always(go):
        go()

    def forward_pair(step, carry):
        forward_block(2 * step, a3a, a3b, 0, lambda go: pl.when(step > 0)(go), always)
        forward_block(2 * step + 1, a3b, a3a, 1, always, lambda go: pl.when(step < 7)(go))
        return carry

    lax.fori_loop(0, BLOCKS // 2, forward_pair, 0)

    for group in range(2):
        for hop in range(4):
            for copy in weight_copies(group, hop):
                copy.wait_send()
    for block in range(BLOCKS):
        @pl.when(relayed_here(block))
        def _(block=block):
            for copy in relay_copies(block):
                copy.wait_send()

    for local in range(PLANES):
        act[local * NZ : (local + 1) * NZ, :] = tiles[globally(local), 1].astype(F32)

    def backward_prep(pg, block, first, count):
        rows = slice(first * NZ, (first + count) * NZ)
        grad = jnp.dot(act[rows, :].astype(BF16), mb_ref[block], preferred_element_type=F32)
        pg[(first + 1) * NZ : (first + 1 + count) * NZ, :] = (
            grad * slope[block, rows, :].astype(F32)
        ).astype(BF16)

    def backward_planes(pg, block, first, count):
        rows = slice(first * NZ, (first + count) * NZ)
        spread = (
            lax.dot_general(
                pg[rows_of(first + 1 + sign, count), :], w_ref[block, 0:384], NT,
                preferred_element_type=F32,
            )
            + lax.dot_general(
                pg[(first + 1) * NZ : (first + 1 + count) * NZ, :], w_ref[block, 384:768], NT,
                preferred_element_type=F32,
            )
            + lax.dot_general(
                pg[rows_of(first + 1 - sign, count), :], w_ref[block, 768:1152], NT,
                preferred_element_type=F32,
            )
        )
        act[rows, :] = act[rows, :] + (
            shifted(spread[:, 0:128], 1) + spread[:, 128:256] + shifted(spread[:, 256:384], -1)
        )

    def grad_copy(buf, par):
        return pltpu.make_async_remote_copy(
            src_ref=buf.at[pl.ds(NZ, NZ)],
            dst_ref=buf.at[pl.ds(0, NZ)],
            send_sem=bsend.at[par],
            recv_sem=brecv.at[par],
            device_id={"section": partner},
            device_id_type=MESH,
        )

    def part_rows(index):
        return pl.ds(pl.multiple_of(index * PART, PART), PART)

    def part_copy(step):
        to = lax.rem(section + step, SECTIONS)
        return pltpu.make_async_remote_copy(
            src_ref=gsend.at[part_rows(to)],
            dst_ref=gparts.at[step],
            send_sem=psend.at[step],
            recv_sem=precv.at[step],
            device_id={"section": to},
            device_id_type=MESH,
        )

    owner = lax.rem(mine, SECTIONS)
    place = (mine - owner) + section

    def home_copy(step, slot):
        return pltpu.make_async_remote_copy(
            src_ref=chunk,
            dst_ref=home.at[slot],
            send_sem=hsend.at[step],
            recv_sem=hrecv.at[slot],
            device_id={"section": owner, "space": lax.rem(mine + step, SPACES)},
            device_id_type=MESH,
        )

    def finish_parts():
        total = grad[part_rows(section), :]
        for step in range(1, SECTIONS):
            part_copy(step).wait_recv()
            total = total + gparts[step].astype(F32)
        chunk[...] = (total * FACTOR).astype(BF16)
        for step in range(1, SPACES):
            home_copy(step, place).start()

        @pl.when(section != owner)
        def _():
            home_copy(0, place).start()

        @pl.when(section == owner)
        def _():
            home[place] = chunk[...]

    def backward_block(block, pg, par, last):
        backward_prep(pg, block, 0, 1)
        last(lambda: grad_copy(pg, par).start())
        for first, count in BWD_CHUNKS:
            backward_prep(pg, block, first, count)

        @pl.when(block == mine)
        def _():
            own = pg[NZ : 9 * NZ, :]
            for dx in range(3):
                term = lax.dot_general(
                    sa3[rows_of(1 + (dx - 1) * sign, PLANES), :], own, TN,
                    preferred_element_type=F32,
                )
                for dz in range(3):
                    first = term[dz * KC : dz * KC + 64]
                    second = term[dz * KC + 64 : (dz + 1) * KC]
                    folded = (first[:, KC:], first[:, :KC] + second[:, KC:], second[:, :KC])
                    for dy in range(3):
                        tap = 9 * dx + 3 * dy + dz
                        grad[tap * 64 : (tap + 1) * 64, :] = folded[dy]
            term = lax.dot_general(
                act[...].astype(BF16), shid[...], TN, preferred_element_type=F32
            )
            grad[TAPS_ROWS:GRAD_ROWS, :] = term[0:64, :KC] + term[64:128, KC:]
            gsend[...] = grad[...].astype(BF16)
            for step in range(1, SECTIONS):
                part_copy(step).start()

        def rest():
            for first, count in BWD_CHUNKS:
                backward_planes(pg, block, first, count)
            grad_copy(pg, par).wait()
            backward_planes(pg, block, 0, 1)

        last(rest)
        pl.when(block == mine - 2)(finish_parts)

    def backward_pair(step, carry):
        backward_block(15 - 2 * step, pga, 0, always)
        backward_block(14 - 2 * step, pgb, 1, lambda go: pl.when(step < 7)(go))
        return carry

    lax.fori_loop(0, BLOCKS // 2, backward_pair, 0)

    @pl.when(needed)
    def _():
        for step in range(1, SPACES):
            tile_copy(step, mine).wait_send()

    pl.when(mine < 2)(finish_parts)

    for step in range(1, SECTIONS):
        part_copy(step).wait_send()

    for slot in range(2 * SECTIONS):
        group, part = slot // SECTIONS, slot % SECTIONS
        here = jnp.logical_and(section == part, mine == group * SECTIONS + section)
        pl.when(jnp.logical_not(here))(lambda slot=slot: home_copy(1, slot).wait_recv())
        value = home[slot].astype(F32)
        rows = min(TAPS_ROWS - part * PART, PART)
        conv_ref[group, part * PART : part * PART + rows, :] = value[:rows]
        if rows < PART:
            mix_ref[group] = value[rows:]

    for step in range(1, SPACES):
        home_copy(step, place).wait_send()
    pl.when(section != owner)(lambda: home_copy(0, place).wait_send())


def run_chain(tile, w, mix):
    vmem = pl.BlockSpec(memory_space=pltpu.VMEM)
    return pl.pallas_call(
        chain_kernel,
        out_shape=(
            jax.ShapeDtypeStruct((2, TAPS_ROWS, 128), F32),
            jax.ShapeDtypeStruct((2, 64, 128), F32),
        ),
        in_specs=[vmem] * 3,
        out_specs=(vmem, vmem),
        scratch_shapes=[
            pltpu.VMEM((10 * NZ, 3 * KC), BF16),
            pltpu.VMEM((10 * NZ, 3 * KC), BF16),
            pltpu.VMEM((PLANES * NZ, KC), F32),
            pltpu.VMEM((BLOCKS, PLANES * NZ, HC), BF16),
            pltpu.VMEM((10 * NZ, 3 * KC), BF16),
            pltpu.VMEM((PLANES * NZ, HC), BF16),
            pltpu.VMEM((10 * NZ, HC), BF16),
            pltpu.VMEM((10 * NZ, HC), BF16),
            pltpu.VMEM((SPACES, 2, NZ, KC), BF16),
            pltpu.VMEM((GRAD_ROWS, 128), F32),
            pltpu.VMEM((GRAD_ROWS, 128), BF16),
            pltpu.VMEM((SECTIONS, PART, 128), BF16),
            pltpu.VMEM((PART, 128), BF16),
            pltpu.VMEM((2 * SECTIONS, PART, 128), BF16),
            pltpu.VMEM((BLOCKS, TAPS_ROWS, 128), BF16),
            pltpu.VMEM((BLOCKS, 64, 128), BF16),
            pltpu.VMEM((BLOCKS, 9 * KC, HC), BF16),
            pltpu.VMEM((BLOCKS, KC, HC), BF16),
            pltpu.SemaphoreType.DMA((2,)),
            pltpu.SemaphoreType.DMA((2,)),
            pltpu.SemaphoreType.DMA((2,)),
            pltpu.SemaphoreType.DMA((2,)),
            pltpu.SemaphoreType.DMA((SPACES,)),
            pltpu.SemaphoreType.DMA((SPACES,)),
            pltpu.SemaphoreType.DMA((SECTIONS,)),
            pltpu.SemaphoreType.DMA((SECTIONS,)),
            pltpu.SemaphoreType.DMA((SPACES,)),
            pltpu.SemaphoreType.DMA((2 * SECTIONS,)),
            pltpu.SemaphoreType.DMA((2, 4)),
            pltpu.SemaphoreType.DMA((2, 4)),
            pltpu.SemaphoreType.DMA((BLOCKS,)),
            pltpu.SemaphoreType.DMA((BLOCKS,)),
            pltpu.SemaphoreType.DMA((BLOCKS,)),
            pltpu.SemaphoreType.DMA((BLOCKS,)),
        ],
        compiler_params=pltpu.CompilerParams(
            has_side_effects=True, vmem_limit_bytes=60 * 1024 * 1024
        ),
        name="chain",
    )(tile, w, mix)


def plane_rows(tile):
    return tile[:, 0].transpose(2, 1, 0).reshape(NZ, KC)


def per_device(inputs, cotangent, conv_weight, mix_weight):
    micro = lax.axis_index("section") // 2
    x = plane_rows(lax.dynamic_index_in_dim(inputs, micro, 0, keepdims=False))
    cot = plane_rows(lax.dynamic_index_in_dim(cotangent, micro, 0, keepdims=False))
    w = conv_weight[:, 0].transpose(0, 2, 1)
    conv_grad, mix_grad = run_chain(jnp.stack([x, cot], 0), w, mix_weight[:, 0])
    return conv_grad.transpose(0, 2, 1)[:, None], mix_grad[:, None]


def solution(mesh):
    placed = (
        P(None, None, "space", None, None),
        P(None, None, "space", None, None),
        P(None, "section", None, None),
        P(None, "section", None, None),
    )
    return jax.shard_map(
        per_device,
        mesh=mesh,
        in_specs=placed,
        out_specs=(P(None, "section", None, None), P(None, "section", None, None)),
        check_vma=False,
    )
```

```python
import math

import jax
import jax.numpy as jnp
from jax import lax
from jax.experimental import pallas as pl
from jax.experimental.pallas import tpu as pltpu
from jax.sharding import PartitionSpec as P

NZ = 128
PLANES = 8
BLOCKS = 16
KC = 128
HC = 256
F32 = jnp.float32
BF16 = jnp.bfloat16
MESH = pl.DeviceIdType.MESH
NT = (((1,), (1,)), ((), ()))
TN = (((0,), (0,)), ((), ()))
FWD_CHUNKS = ((1, 2), (3, 2), (5, 3))
BWD_CHUNKS = ((1, 2), (3, 2), (5, 3))
SECTIONS = 8
SPACES = 16
TAPS_ROWS = 1728
GRAD_ROWS = 1792
PART = GRAD_ROWS // SECTIONS
FACTOR = 1.0 / math.sqrt(16384.0)


def rows_of(start, count):
    return pl.ds(pl.multiple_of(start * NZ, NZ), count * NZ)


def shifted(value, step):
    planes = value.shape[0] // NZ
    rolled = pltpu.roll(value, (-step) % value.shape[0], 0)
    row = lax.broadcasted_iota(jnp.int32, value.shape, 0) % NZ
    edge = NZ - 1 if step == 1 else 0
    return jnp.where(row == edge, 0.0, rolled)


def widen(value):
    return jnp.concatenate(
        [shifted(value, -1).astype(BF16), value.astype(BF16), shifted(value, 1).astype(BF16)], axis=1
    )


def chain_kernel(
    tile_ref, wt_ref, mt_ref,
    conv_ref, mix_ref,
    a3a, a3b, act, slope, sa3, shid, pga, pgb,
    tiles, grad, gsend, gparts, chunk, home,
    wraw, mraw, w_ref, mb_ref,
    fsend, frecv, bsend, brecv,
    tsend, trecv, psend, precv, hsend, hrecv,
    wsend, msend, wrelay, mrelay, wrecv, mrecv,
):
    section = lax.axis_index("section")
    core = lax.rem(section, 2)
    partner = section + 1 - 2 * core
    mine = lax.axis_index("space")
    sign = 2 * core - 1

    def globally(local):
        return 7 + core + sign * local

    def tile_copy(step, slot):
        return pltpu.make_async_remote_copy(
            src_ref=tile_ref,
            dst_ref=tiles.at[slot],
            send_sem=tsend.at[step],
            recv_sem=trecv.at[slot],
            device_id={"space": lax.rem(mine + step, SPACES)},
            device_id_type=MESH,
        )

    needed = jnp.where(core == 0, mine <= 8, mine >= 7)

    @pl.when(needed)
    def _():
        for step in range(1, SPACES):
            tile_copy(step, mine).start()

    def weight_copies(group, hop):
        to = partner if hop == 0 else lax.rem(section + 2 * hop, SECTIONS)
        block = group * SECTIONS + section
        return [
            pltpu.make_async_remote_copy(
                src_ref=src.at[group],
                dst_ref=dst.at[block],
                send_sem=send.at[group, hop],
                recv_sem=recv.at[block],
                device_id={"section": to},
                device_id_type=MESH,
            )
            for src, dst, send, recv in (
                (wt_ref, wraw, wsend, wrecv), (mt_ref, mraw, msend, mrecv)
            )
        ]

    def relay_copies(block):
        return [
            pltpu.make_async_remote_copy(
                src_ref=buf.at[block],
                dst_ref=buf.at[block],
                send_sem=send.at[block],
                recv_sem=recv.at[block],
                device_id={"section": partner},
                device_id_type=MESH,
            )
            for buf, send, recv in ((wraw, wrelay, wrecv), (mraw, mrelay, mrecv))
        ]

    for group in range(2):
        for hop in (0, 1, 3, 2):
            for copy in weight_copies(group, hop):
                copy.start()
        wraw[group * SECTIONS + section] = wt_ref[group]
        mraw[group * SECTIONS + section] = mt_ref[group]

    def relayed_here(block):
        return jnp.logical_and(lax.rem(block, 2) == core, lax.rem(block, SECTIONS) != section)

    def pass_on(block):
        @pl.when(relayed_here(block))
        def _():
            for copy in relay_copies(block):
                copy.wait_recv()
            for copy in relay_copies(block):
                copy.start()

    def expand(block):
        @pl.when(lax.rem(block, 2) != core)
        def _():
            for copy in relay_copies(block):
                copy.wait_recv()

        for dx in range(3):
            for dz in range(3):
                row = (3 * dx + dz) * KC
                low, mid, high = (
                    wraw[block, (9 * dx + 3 * dy + dz) * 64 : (9 * dx + 3 * dy + dz + 1) * 64, :]
                    for dy in range(3)
                )
                w_ref[block, row : row + 64, 0:128] = mid
                w_ref[block, row : row + 64, 128:256] = low
                w_ref[block, row + 64 : row + 128, 0:128] = high
                w_ref[block, row + 64 : row + 128, 128:256] = mid
        empty = jnp.zeros((64, 128), BF16)
        mb_ref[block, 0:64, 0:128] = mraw[block]
        mb_ref[block, 0:64, 128:256] = empty
        mb_ref[block, 64:128, 0:128] = empty
        mb_ref[block, 64:128, 128:256] = mraw[block]

    tiles[mine] = tile_ref[...]
    pass_on(0)
    pass_on(1)

    zeros3 = jnp.zeros((NZ, 3 * KC), BF16)
    for a3 in (a3a, a3b):
        a3[9 * NZ : 10 * NZ, :] = zeros3
    for pg in (pga, pgb):
        pg[9 * NZ : 10 * NZ, :] = jnp.zeros((NZ, HC), BF16)
    for local in range(-1, PLANES):
        plane = globally(local)
        pl.when(plane != mine)(lambda plane=plane: tile_copy(1, plane).wait_recv())
        tile = tiles[plane, 0].astype(F32)
        if local >= 0:
            act[local * NZ : (local + 1) * NZ, :] = tile
        a3a[(local + 1) * NZ : (local + 2) * NZ, :] = widen(tile)

    def forward_planes(cur, nxt, block, first, count):
        rows = slice(first * NZ, (first + count) * NZ)
        window = jnp.concatenate(
            [
                cur[rows_of(first + 1 - sign, count), :],
                cur[(first + 1) * NZ : (first + 1 + count) * NZ, :],
                cur[rows_of(first + 1 + sign, count), :],
            ],
            axis=1,
        )
        pre = jnp.dot(window, w_ref[block], preferred_element_type=F32)
        sg = 0.5 + 0.5 * jnp.tanh(0.5 * pre)
        hid = pre * sg
        slope[block, rows, :] = (sg + hid * (1.0 - sg)).astype(BF16)
        hid = hid.astype(BF16)

        @pl.when(block == mine)
        def _():
            shid[rows, :] = hid

        new = act[rows, :] + lax.dot_general(
            hid, mb_ref[block], NT, preferred_element_type=F32
        )
        act[rows, :] = new
        nxt[(first + 1) * NZ : (first + 1 + count) * NZ, :] = widen(new)

    def act_copy(buf, par):
        return pltpu.make_async_remote_copy(
            src_ref=buf.at[pl.ds(NZ, NZ)],
            dst_ref=buf.at[pl.ds(0, NZ)],
            send_sem=fsend.at[par],
            recv_sem=frecv.at[par],
            device_id={"section": partner},
            device_id_type=MESH,
        )

    def forward_block(block, cur, nxt, par, wait, send):
        expand(block)
        for first, count in FWD_CHUNKS:
            forward_planes(cur, nxt, block, first, count)
        wait(lambda: act_copy(cur, par).wait())

        @pl.when(block == mine)
        def _():
            sa3[...] = cur[...]

        forward_planes(cur, nxt, block, 0, 1)
        send(lambda: act_copy(nxt, 1 - par).start())
        pl.when(block < BLOCKS - 2)(lambda: pass_on(block + 2))

    def always(go):
        go()

    def forward_pair(step, carry):
        forward_block(2 * step, a3a, a3b, 0, lambda go: pl.when(step > 0)(go), always)
        forward_block(2 * step + 1, a3b, a3a, 1, always, lambda go: pl.when(step < 7)(go))
        return carry

    lax.fori_loop(0, BLOCKS // 2, forward_pair, 0)

    for group in range(2):
        for hop in range(4):
            for copy in weight_copies(group, hop):
                copy.wait_send()
    for block in range(BLOCKS):
        @pl.when(relayed_here(block))
        def _(block=block):
            for copy in relay_copies(block):
                copy.wait_send()

    for local in range(PLANES):
        act[local * NZ : (local + 1) * NZ, :] = tiles[globally(local), 1].astype(F32)

    def backward_prep(pg, block, first, count):
        rows = slice(first * NZ, (first + count) * NZ)
        grad = jnp.dot(act[rows, :].astype(BF16), mb_ref[block], preferred_element_type=F32)
        pg[(first + 1) * NZ : (first + 1 + count) * NZ, :] = (
            grad * slope[block, rows, :].astype(F32)
        ).astype(BF16)

    def backward_planes(pg, block, first, count):
        rows = slice(first * NZ, (first + count) * NZ)
        spread = (
            lax.dot_general(
                pg[rows_of(first + 1 + sign, count), :], w_ref[block, 0:384], NT,
                preferred_element_type=F32,
            )
            + lax.dot_general(
                pg[(first + 1) * NZ : (first + 1 + count) * NZ, :], w_ref[block, 384:768], NT,
                preferred_element_type=F32,
            )
            + lax.dot_general(
                pg[rows_of(first + 1 - sign, count), :], w_ref[block, 768:1152], NT,
                preferred_element_type=F32,
            )
        )
        act[rows, :] = act[rows, :] + (
            shifted(spread[:, 0:128], 1) + spread[:, 128:256] + shifted(spread[:, 256:384], -1)
        )

    def grad_copy(buf, par):
        return pltpu.make_async_remote_copy(
            src_ref=buf.at[pl.ds(NZ, NZ)],
            dst_ref=buf.at[pl.ds(0, NZ)],
            send_sem=bsend.at[par],
            recv_sem=brecv.at[par],
            device_id={"section": partner},
            device_id_type=MESH,
        )

    def part_rows(index):
        return pl.ds(pl.multiple_of(index * PART, PART), PART)

    def part_copy(step):
        to = lax.rem(section + step, SECTIONS)
        return pltpu.make_async_remote_copy(
            src_ref=gsend.at[part_rows(to)],
            dst_ref=gparts.at[step],
            send_sem=psend.at[step],
            recv_sem=precv.at[step],
            device_id={"section": to},
            device_id_type=MESH,
        )

    owner = lax.rem(mine, SECTIONS)
    place = (mine - owner) + section

    def home_copy(step, slot):
        return pltpu.make_async_remote_copy(
            src_ref=chunk,
            dst_ref=home.at[slot],
            send_sem=hsend.at[step],
            recv_sem=hrecv.at[slot],
            device_id={"section": owner, "space": lax.rem(mine + step, SPACES)},
            device_id_type=MESH,
        )

    def finish_parts():
        total = grad[part_rows(section), :]
        for step in range(1, SECTIONS):
            part_copy(step).wait_recv()
            total = total + gparts[step].astype(F32)
        chunk[...] = (total * FACTOR).astype(BF16)
        for step in range(1, SPACES):
            home_copy(step, place).start()

        @pl.when(section != owner)
        def _():
            home_copy(0, place).start()

        @pl.when(section == owner)
        def _():
            home[place] = chunk[...]

    def backward_block(block, pg, par, last):
        backward_prep(pg, block, 0, 1)
        last(lambda: grad_copy(pg, par).start())
        for first, count in BWD_CHUNKS:
            backward_prep(pg, block, first, count)

        @pl.when(block == mine)
        def _():
            own = pg[NZ : 9 * NZ, :]
            for dx in range(3):
                term = lax.dot_general(
                    sa3[rows_of(1 + (dx - 1) * sign, PLANES), :], own, TN,
                    preferred_element_type=F32,
                )
                for dz in range(3):
                    first = term[dz * KC : dz * KC + 64]
                    second = term[dz * KC + 64 : (dz + 1) * KC]
                    folded = (first[:, KC:], first[:, :KC] + second[:, KC:], second[:, :KC])
                    for dy in range(3):
                        tap = 9 * dx + 3 * dy + dz
                        grad[tap * 64 : (tap + 1) * 64, :] = folded[dy]
            term = lax.dot_general(
                act[...].astype(BF16), shid[...], TN, preferred_element_type=F32
            )
            grad[TAPS_ROWS:GRAD_ROWS, :] = term[0:64, :KC] + term[64:128, KC:]
            gsend[...] = grad[...].astype(BF16)
            for step in range(1, SECTIONS):
                part_copy(step).start()

        def rest():
            for first, count in BWD_CHUNKS:
                backward_planes(pg, block, first, count)
            grad_copy(pg, par).wait()
            backward_planes(pg, block, 0, 1)

        last(rest)
        pl.when(block == mine - 2)(finish_parts)

    def backward_pair(step, carry):
        backward_block(15 - 2 * step, pga, 0, always)
        backward_block(14 - 2 * step, pgb, 1, lambda go: pl.when(step < 7)(go))
        return carry

    lax.fori_loop(0, BLOCKS // 2, backward_pair, 0)

    @pl.when(needed)
    def _():
        for step in range(1, SPACES):
            tile_copy(step, mine).wait_send()

    pl.when(mine < 2)(finish_parts)

    for step in range(1, SECTIONS):
        part_copy(step).wait_send()

    for slot in range(2 * SECTIONS):
        group, part = slot // SECTIONS, slot % SECTIONS
        here = jnp.logical_and(section == part, mine == group * SECTIONS + section)
        pl.when(jnp.logical_not(here))(lambda slot=slot: home_copy(1, slot).wait_recv())
        value = home[slot]
        rows = min(TAPS_ROWS - part * PART, PART)
        conv_ref[group, part * PART : part * PART + rows, :] = value[:rows]
        if rows < PART:
            mix_ref[group] = value[rows:]

    for step in range(1, SPACES):
        home_copy(step, place).wait_send()
    pl.when(section != owner)(lambda: home_copy(0, place).wait_send())


def run_chain(tile, w, mix):
    vmem = pl.BlockSpec(memory_space=pltpu.VMEM)
    return pl.pallas_call(
        chain_kernel,
        out_shape=(
            jax.ShapeDtypeStruct((2, TAPS_ROWS, 128), BF16),
            jax.ShapeDtypeStruct((2, 64, 128), BF16),
        ),
        in_specs=[vmem] * 3,
        out_specs=(vmem, vmem),
        scratch_shapes=[
            pltpu.VMEM((10 * NZ, 3 * KC), BF16),
            pltpu.VMEM((10 * NZ, 3 * KC), BF16),
            pltpu.VMEM((PLANES * NZ, KC), F32),
            pltpu.VMEM((BLOCKS, PLANES * NZ, HC), BF16),
            pltpu.VMEM((10 * NZ, 3 * KC), BF16),
            pltpu.VMEM((PLANES * NZ, HC), BF16),
            pltpu.VMEM((10 * NZ, HC), BF16),
            pltpu.VMEM((10 * NZ, HC), BF16),
            pltpu.VMEM((SPACES, 2, NZ, KC), BF16),
            pltpu.VMEM((GRAD_ROWS, 128), F32),
            pltpu.VMEM((GRAD_ROWS, 128), BF16),
            pltpu.VMEM((SECTIONS, PART, 128), BF16),
            pltpu.VMEM((PART, 128), BF16),
            pltpu.VMEM((2 * SECTIONS, PART, 128), BF16),
            pltpu.VMEM((BLOCKS, TAPS_ROWS, 128), BF16),
            pltpu.VMEM((BLOCKS, 64, 128), BF16),
            pltpu.VMEM((BLOCKS, 9 * KC, HC), BF16),
            pltpu.VMEM((BLOCKS, KC, HC), BF16),
            pltpu.SemaphoreType.DMA((2,)),
            pltpu.SemaphoreType.DMA((2,)),
            pltpu.SemaphoreType.DMA((2,)),
            pltpu.SemaphoreType.DMA((2,)),
            pltpu.SemaphoreType.DMA((SPACES,)),
            pltpu.SemaphoreType.DMA((SPACES,)),
            pltpu.SemaphoreType.DMA((SECTIONS,)),
            pltpu.SemaphoreType.DMA((SECTIONS,)),
            pltpu.SemaphoreType.DMA((SPACES,)),
            pltpu.SemaphoreType.DMA((2 * SECTIONS,)),
            pltpu.SemaphoreType.DMA((2, 4)),
            pltpu.SemaphoreType.DMA((2, 4)),
            pltpu.SemaphoreType.DMA((BLOCKS,)),
            pltpu.SemaphoreType.DMA((BLOCKS,)),
            pltpu.SemaphoreType.DMA((BLOCKS,)),
            pltpu.SemaphoreType.DMA((BLOCKS,)),
        ],
        compiler_params=pltpu.CompilerParams(
            has_side_effects=True, vmem_limit_bytes=60 * 1024 * 1024
        ),
        name="chain",
    )(tile, w, mix)


def plane_rows(tile):
    return tile[:, 0].transpose(2, 1, 0).reshape(NZ, KC)


def per_device(inputs, cotangent, conv_weight, mix_weight):
    micro = lax.axis_index("section") // 2
    x = plane_rows(lax.dynamic_index_in_dim(inputs, micro, 0, keepdims=False))
    cot = plane_rows(lax.dynamic_index_in_dim(cotangent, micro, 0, keepdims=False))
    w = conv_weight[:, 0].transpose(0, 2, 1)
    conv_grad, mix_grad = run_chain(jnp.stack([x, cot], 0), w, mix_weight[:, 0])
    return (
        conv_grad.astype(F32).transpose(0, 2, 1)[:, None],
        mix_grad.astype(F32)[:, None],
    )


def solution(mesh):
    placed = (
        P(None, None, "space", None, None),
        P(None, None, "space", None, None),
        P(None, "section", None, None),
        P(None, "section", None, None),
    )
    return jax.shard_map(
        per_device,
        mesh=mesh,
        in_specs=placed,
        out_specs=(P(None, "section", None, None), P(None, "section", None, None)),
        check_vma=False,
    )
```
